32 devices in a mesh: pp: 2 (over y), cp: 4 (over z), tp: 4 (over x, core).
Axes of the slice: x: 2, y: 2, z: 4, core: 2. Of those that a mesh axis runs over, the one named last changes fastest.
Arguments:
- query_vectors: bfloat16 [2, 768, 4096], P('pp', 'cp', 'tp'), may hold values from -50 to 50
- key_vectors: bfloat16 [2, 768, 4096], P('pp', 'cp', 'tp'), may hold values from -0.5 to 0.5
- value_vectors: bfloat16 [2, 768, 4096], P('pp', 'cp', 'tp'), may hold values from -150 to 150
- section_inputs: bfloat16 [2, 768, 4096], P('pp', 'cp', 'tp'), may hold values from -6 to 6
- top_grad: bfloat16 [768, 4096], P('cp', 'tp'), may hold values from -6 to 6
- out_gains: float32 [2, 4096], P('pp', 'tp'), may hold values from 0.5 to 2
Outputs:
- section_grads: bfloat16 [2, 768, 4096], P('pp', 'cp', 'tp')
- query_grads: bfloat16 [2, 768, 4096], P('pp', 'cp', 'tp')
- key_grads: bfloat16 [2, 768, 4096], P('pp', 'cp', 'tp')
- value_grads: bfloat16 [2, 768, 4096], P('pp', 'cp', 'tp')
The draws below stay inside these ranges and needn't reach their ends.
All inputs are finite; a program needn't handle non-finite values.
Results may differ from the reference program's by a relative error of at most 0.01.
Values may be sent and summed in bfloat16 or wider, within the bound.
A program may use at most 64 MiB of HBM per device.

```python
import math
import jax
import jax.numpy as jnp
from jax import lax

HEADS = 32
HEAD = 128
WIDTH = 4096
TOK_DEV = 192
TOKENS = 768
LAYERS = 2


def draw_query_vectors(key, part):
    base_key, scale_key = jax.random.split(jax.random.fold_in(key, 11))
    base = jnp.clip(jax.random.normal(base_key, (LAYERS, TOKENS, WIDTH), jnp.float32), -5.0, 5.0)
    row_scale = jnp.exp(jax.random.uniform(scale_key, (LAYERS, TOKENS, 1), jnp.float32, 0.0, math.log(10.0)))
    return (base * row_scale).astype(jnp.bfloat16)


def draw_value_vectors(key, part):
    base_key, column_key = jax.random.split(jax.random.fold_in(key, 23), 2)
    head_index = (jnp.arange(WIDTH) // HEAD).astype(jnp.float32)
    rising = jnp.exp(head_index * (math.log(3.0) / max(HEADS - 1, 1)))
    column_scale = jnp.exp(jax.random.uniform(column_key, (LAYERS, 1, WIDTH), jnp.float32, 0.0, math.log(10.0))) * rising
    base = jnp.clip(jax.random.normal(base_key, (LAYERS, TOKENS, WIDTH), jnp.float32), -5.0, 5.0)
    return (base * column_scale).astype(jnp.bfloat16)


def shard_levels(key, extent, cuts, low, largest):
    def one(position, blocks):
        heights = jax.random.uniform(jax.random.fold_in(jax.random.fold_in(key, 6), position), (blocks,), jnp.float32, low / len(cuts), largest / len(cuts))
        return jnp.repeat(jnp.exp(heights), extent[position] // blocks).reshape((-1,) + (1,) * (len(extent) - position - 1))

    level = one(*cuts[0])
    for cut in cuts[1:]:
        level = level * one(*cut)
    return level


def centred(key, extent, scale, most, shards=(), held_as=jnp.bfloat16):
    values = scale * jax.random.normal(key, extent, jnp.float32)
    if shards:
        values = values * shard_levels(key, extent, shards, -0.22, 0.18)
    return jnp.clip(values, -most, most).astype(held_as)


def setup_inputs(seed: int = 0) -> dict:
    splits = jax.random.split(jax.random.key(seed), 7)
    return {
        "query_vectors": draw_query_vectors(jax.random.fold_in(splits[6], 71), 0),
        "key_vectors": centred(splits[1], (LAYERS, TOKENS, WIDTH), HEAD ** -0.5, 0.5, ((0, 2), (1, 4), (2, 4))),
        "value_vectors": draw_value_vectors(jax.random.fold_in(splits[6], 71), 0),
        "section_inputs": centred(splits[3], (LAYERS, TOKENS, WIDTH), 1.5, 6.0, ((0, 2), (1, 4), (2, 4))),
        "top_grad": centred(splits[4], (TOKENS, WIDTH), 1.0, 6.0, ((0, 4), (1, 4))),
        "out_gains": jnp.clip(jnp.exp(math.log(2.0) - 1.3862944 * jax.random.uniform(splits[5], (LAYERS, WIDTH), jnp.float32) ** shard_levels(splits[5], (LAYERS, WIDTH), ((0, 2), (1, 4)), -0.2, 0.2)), 0.5, 2.0),
    }


EPSILON = 1e-06

def rounded(array):
    return lax.optimization_barrier(array.astype(jnp.bfloat16)).astype(jnp.float32)

def layer_grads(query_layer, key_layer, value_layer, section_input, out_gain, top_grad, later_product):
    blocks = TOKENS // TOK_DEV
    block_shape = (blocks, TOK_DEV, HEADS, HEAD)
    query_blocks = query_layer.astype(jnp.float32).reshape(block_shape)
    key_blocks = key_layer.astype(jnp.float32).reshape(block_shape)
    value_blocks = value_layer.astype(jnp.float32).reshape(block_shape)
    causal = jnp.arange(TOK_DEV)[:, None] >= jnp.arange(TOK_DEV)[None, :]
    local_state = jnp.einsum('bthd,bthe->bhde', key_blocks, value_blocks)
    running = jnp.cumsum(local_state, axis=0)
    prefix = rounded(jnp.concatenate([jnp.zeros_like(local_state[:1]), running[:-1]], axis=0))
    scores = rounded(jnp.where(causal, jnp.einsum('bthd,bshd->bhts', query_blocks, key_blocks), 0.0))
    attention = jnp.einsum('bhts,bshe->bthe', scores, value_blocks) + jnp.einsum('bthd,bhde->bthe', query_blocks, prefix)
    attention = attention.reshape(TOKENS, WIDTH)
    scale_root = jnp.sqrt(lax.optimization_barrier(jnp.mean(attention * attention, axis=1, keepdims=True)) + EPSILON)
    normed = attention / scale_root
    sigmoid_gate = jax.nn.sigmoid(section_input.astype(jnp.float32))
    factor = 1.0 + out_gain * normed * sigmoid_gate * (1.0 - sigmoid_gate)
    incoming_grad = top_grad.astype(jnp.float32) * later_product
    section_grad = (incoming_grad * factor).astype(jnp.bfloat16)
    normed_grad = incoming_grad * out_gain * sigmoid_gate
    inner_mean = lax.optimization_barrier(jnp.mean(normed_grad * normed, axis=1, keepdims=True))
    attention_grad = rounded((normed_grad - normed * inner_mean) / scale_root).reshape(block_shape)
    grad_state = jnp.einsum('bthd,bthe->bhde', query_blocks, attention_grad)
    behind = jnp.cumsum(grad_state[::-1], axis=0)[::-1]
    suffix = rounded(jnp.concatenate([behind[1:], jnp.zeros_like(grad_state[:1])], axis=0))
    score_grad = rounded(jnp.where(causal, jnp.einsum('bthe,bshe->bhts', attention_grad, value_blocks), 0.0))
    query_grad = jnp.einsum('bhts,bshd->bthd', score_grad, key_blocks) + jnp.einsum('bthe,bhde->bthd', attention_grad, prefix)
    key_grad = jnp.einsum('bhts,bthd->bshd', score_grad, query_blocks) + jnp.einsum('bshe,bhde->bshd', value_blocks, suffix)
    value_grad = jnp.einsum('bhts,bthe->bshe', scores, attention_grad) + jnp.einsum('bshd,bhde->bshe', key_blocks, suffix)
    query_grad = query_grad.reshape(TOKENS, WIDTH).astype(jnp.bfloat16)
    key_grad = key_grad.reshape(TOKENS, WIDTH).astype(jnp.bfloat16)
    value_grad = value_grad.reshape(TOKENS, WIDTH).astype(jnp.bfloat16)
    return (factor, section_grad, query_grad, key_grad, value_grad)

def reference(query_vectors, key_vectors, value_vectors, section_inputs, top_grad, out_gains):
    later_product = jnp.ones((TOKENS, WIDTH), jnp.float32)
    section_list = []
    query_list = []
    key_list = []
    value_list = []
    for section_index in range(LAYERS - 1, -1, -1):
        factor, section_grad, query_grad, key_grad, value_grad = layer_grads(query_vectors[section_index], key_vectors[section_index], value_vectors[section_index], section_inputs[section_index], out_gains[section_index][None, :], top_grad, later_product)
        section_list.insert(0, section_grad)
        query_list.insert(0, query_grad)
        key_list.insert(0, key_grad)
        value_list.insert(0, value_grad)
        later_product = later_product * factor
    return (jnp.stack(section_list), jnp.stack(query_list), jnp.stack(key_list), jnp.stack(value_list))
```

```python
import functools

import jax
import jax.numpy as jnp
from jax import lax
from jax.experimental import pallas as pl
from jax.experimental.pallas import tpu as pltpu
from jax.sharding import PartitionSpec as P

HEAD = 128
LANES = 128
EPSILON = 1e-06
MESH = pl.DeviceIdType.MESH
F32 = jnp.float32
BF16 = jnp.bfloat16


def dot(a, b, a_dim, b_dim):
    return lax.dot_general(a, b, (((a_dim,), (b_dim,)), ((), ())), preferred_element_type=F32)


def kernel(
    sizes,
    q_hbm, k_hbm, v_hbm, x_hbm, top_hbm, gain_hbm,
    sec_hbm, qg_hbm, kg_hbm, vg_hbm,
    q, k, v, x, top, gain, sec, qg, kg, vg,
    pre_in, pre_out, suf_in, suf_out, states, scores, att, ng, gate, ag, b_out, b_in,
    rows_out, rows_in, inv_out, inv_in,
    in_sem, sec_sem, out_sem, pre_send, pre_recv, suf_send, suf_recv,
    b_send, b_recv, row_send, row_recv, inv_send, inv_recv,
):
    layers, blocks, shards = sizes
    p, c, t = lax.axis_index("pp"), lax.axis_index("cp"), lax.axis_index("tp")
    rows, width = q.shape
    heads = width // HEAD
    padded = rows_out.shape[2]
    total_width = width * shards

    def cols(h):
        return slice(h * HEAD, (h + 1) * HEAD)

    loads = [
        pltpu.make_async_copy(k_hbm.at[0], k, in_sem.at[0]),
        pltpu.make_async_copy(v_hbm.at[0], v, in_sem.at[1]),
        pltpu.make_async_copy(q_hbm.at[0], q, in_sem.at[2]),
        pltpu.make_async_copy(x_hbm.at[0], x, in_sem.at[3]),
        pltpu.make_async_copy(gain_hbm, gain, in_sem.at[4]),
        pltpu.make_async_copy(top_hbm, top, in_sem.at[5]),
    ]
    for load in loads:
        load.start()

    barrier = pltpu.get_barrier_semaphore()

    @pl.when(c > 0)
    def _():
        pl.semaphore_signal(barrier, inc=1, device_id={"cp": c - 1}, device_id_type=MESH)

    @pl.when(c < blocks - 1)
    def _():
        pl.semaphore_signal(barrier, inc=1, device_id={"cp": c + 1}, device_id_type=MESH)

    for d in range(1, shards):
        pl.semaphore_signal(
            barrier, inc=1, device_id={"tp": lax.rem(t + d, shards)}, device_id_type=MESH
        )
    for d in range(1, layers):
        pl.semaphore_signal(
            barrier, inc=1, device_id={"pp": lax.rem(p + d, layers)}, device_id_type=MESH
        )

    @pl.when(c == 0)
    def _():
        pre_in[...] = jnp.zeros_like(pre_in)

    @pl.when(c == blocks - 1)
    def _():
        suf_in[...] = jnp.zeros_like(suf_in)

    for d in range(1, layers):

        @pl.when(p + d >= layers)
        def _():
            b_in[d - 1] = jnp.zeros(b_in.shape[1:], b_in.dtype)
            inv_in[d - 1] = jnp.zeros(inv_in.shape[1:], inv_in.dtype)

    def pre_copy(h):
        return pltpu.make_async_remote_copy(
            src_ref=pre_out.at[h], dst_ref=pre_in.at[h],
            send_sem=pre_send.at[h], recv_sem=pre_recv.at[h],
            device_id={"cp": c + 1}, device_id_type=MESH,
        )

    def suf_copy(h):
        return pltpu.make_async_remote_copy(
            src_ref=suf_out.at[h], dst_ref=suf_in.at[h],
            send_sem=suf_send.at[h], recv_sem=suf_recv.at[h],
            device_id={"cp": c - 1}, device_id_type=MESH,
        )

    def b_copy(d, h):
        return pltpu.make_async_remote_copy(
            src_ref=b_out.at[h], dst_ref=b_in.at[d - 1, h],
            send_sem=b_send.at[d - 1, h], recv_sem=b_recv.at[d - 1, h],
            device_id={"pp": p - d}, device_id_type=MESH,
        )

    def inv_copy(d):
        return pltpu.make_async_remote_copy(
            src_ref=inv_out, dst_ref=inv_in.at[d - 1],
            send_sem=inv_send.at[d - 1], recv_sem=inv_recv.at[d - 1],
            device_id={"pp": p - d}, device_id_type=MESH,
        )

    def row_copy(i, d):
        return pltpu.make_async_remote_copy(
            src_ref=rows_out.at[i], dst_ref=rows_in.at[i, d - 1],
            send_sem=row_send.at[i, d - 1], recv_sem=row_recv.at[i, d - 1],
            device_id={"tp": lax.rem(t + d, shards)}, device_id_type=MESH,
        )

    def to_row(partial):
        if padded > rows:
            fill = jnp.zeros((padded - rows, LANES), F32)
            partial = jnp.concatenate([partial, fill], axis=0)
        return jnp.broadcast_to(jnp.sum(partial.T, axis=0, keepdims=True), (8, padded))

    def to_col(row):
        return jnp.broadcast_to(row[0:1], (LANES, padded)).T[:rows]

    def row_start(i, partial):
        rows_out[i] = to_row(partial)
        for d in range(1, shards):
            row_copy(i, d).start()

    def row_finish(i):
        total = rows_out[i]
        for d in range(1, shards):
            row_copy(i, d).wait_recv()
            total = total + rows_in[i, d - 1]
        return total

    causal = lax.broadcasted_iota(jnp.int32, (rows, rows), 0) >= lax.broadcasted_iota(
        jnp.int32, (rows, rows), 1
    )
    inner = jnp.logical_and(c > 0, c < blocks - 1)

    partners = (shards - 1) + (layers - 1)
    pl.semaphore_wait(
        barrier, partners + jnp.where(c > 0, 1, 0) + jnp.where(c < blocks - 1, 1, 0)
    )

    loads[0].wait()
    loads[1].wait()
    for h in range(heads):
        state = dot(k[:, cols(h)], v[:, cols(h)], 0, 0)
        states[h] = state
        if blocks > 1:

            @pl.when(c == 0)
            def _():
                pre_out[h] = state.astype(BF16)
                pre_copy(h).start()

    for load in loads[2:5]:
        load.wait()
    squares = jnp.zeros((rows, LANES), F32)
    for h in range(heads):
        query, value = q[:, cols(h)], v[:, cols(h)]
        score = jnp.where(causal, dot(query, k[:, cols(h)], 1, 1), 0.0).astype(BF16)
        scores[h] = score
        attention = dot(score, value, 1, 0)
        sig = jax.nn.sigmoid(x[:, cols(h)].astype(F32))
        gate[:, cols(h)] = sig

        if blocks > 1:

            @pl.when(c > 0)
            def _():
                pre_copy(h).wait_recv()

            @pl.when(inner)
            def _():
                pre_out[h] = (pre_in[h].astype(F32) + states[h]).astype(BF16)
                pre_copy(h).start()

        attention = attention + dot(query, pre_in[h], 1, 0)
        att[:, cols(h)] = attention
        squares = squares + attention * attention
        if layers > 1:
            b_out[h] = (attention * (gain[:, cols(h)] * sig * (1.0 - sig))).astype(BF16)
            for d in range(1, layers):

                @pl.when(p >= d)
                def _():
                    b_copy(d, h).start()

    row_start(0, squares)
    loads[5].wait()
    inv_row = 1.0 / jnp.sqrt(row_finish(0) / total_width + EPSILON)
    inv_out[...] = inv_row
    for d in range(1, layers):

        @pl.when(p >= d)
        def _():
            inv_copy(d).start()

    inv = to_col(inv_row)
    for d in range(1, layers):

        @pl.when(p + d < layers)
        def _():
            inv_copy(d).wait_recv()

    later_inv = [to_col(inv_in[d - 1]) for d in range(1, layers)]
    products = jnp.zeros((rows, LANES), F32)
    for h in range(heads):
        normed = att[:, cols(h)] * inv
        sig = gate[:, cols(h)]
        scaled = gain[:, cols(h)] * sig
        factor = 1.0 + normed * scaled * (1.0 - sig)
        incoming = top[:, cols(h)].astype(F32)
        for d in range(1, layers):

            @pl.when(p + d < layers)
            def _():
                b_copy(d, h).wait_recv()

            incoming = incoming * (1.0 + b_in[d - 1, h].astype(F32) * later_inv[d - 1])
        sec[:, cols(h)] = (incoming * factor).astype(BF16)
        normed_grad = incoming * scaled
        ng[:, cols(h)] = normed_grad
        att[:, cols(h)] = normed
        products = products + normed_grad * normed

    row_start(1, products)
    sec_copy = pltpu.make_async_copy(sec, sec_hbm.at[0], sec_sem)
    sec_copy.start()
    mean = to_col(row_finish(1) / total_width)
    for h in range(heads):
        grad = ((ng[:, cols(h)] - att[:, cols(h)] * mean) * inv).astype(BF16)
        ag[:, cols(h)] = grad
        state = dot(q[:, cols(h)], grad, 0, 0)
        states[h] = state
        if blocks > 1:

            @pl.when(c == blocks - 1)
            def _():
                suf_out[h] = state.astype(BF16)
                suf_copy(h).start()

    def out_copies(h):
        return [
            pltpu.make_async_copy(
                src.at[:, cols(h)], dst.at[0, :, cols(h)], out_sem.at[i, h]
            )
            for i, (src, dst) in enumerate(((qg, qg_hbm), (kg, kg_hbm), (vg, vg_hbm)))
        ]

    for h in range(heads):
        query, key, value = q[:, cols(h)], k[:, cols(h)], v[:, cols(h)]
        grad = ag[:, cols(h)]
        score_grad = jnp.where(causal, dot(grad, value, 1, 1), 0.0).astype(BF16)
        query_grad = dot(score_grad, key, 1, 0) + dot(grad, pre_in[h], 1, 1)
        qg[:, cols(h)] = query_grad.astype(BF16)
        key_grad = dot(score_grad, query, 0, 0)
        value_grad = dot(scores[h], grad, 0, 0)
        if blocks > 1:

            @pl.when(c < blocks - 1)
            def _():
                suf_copy(h).wait_recv()

            @pl.when(inner)
            def _():
                suf_out[h] = (suf_in[h].astype(F32) + states[h]).astype(BF16)
                suf_copy(h).start()

        suffix = suf_in[h]
        kg[:, cols(h)] = (key_grad + dot(value, suffix, 1, 1)).astype(BF16)
        vg[:, cols(h)] = (value_grad + dot(key, suffix, 1, 0)).astype(BF16)
        for copy in out_copies(h):
            copy.start()

    if blocks > 1:

        @pl.when(c < blocks - 1)
        def _():
            for h in range(heads):
                pre_copy(h).wait_send()

        @pl.when(c > 0)
        def _():
            for h in range(heads):
                suf_copy(h).wait_send()

    for d in range(1, layers):

        @pl.when(p >= d)
        def _():
            inv_copy(d).wait_send()
            for h in range(heads):
                b_copy(d, h).wait_send()

    for i in range(2):
        for d in range(1, shards):
            row_copy(i, d).wait_send()
    sec_copy.wait()
    for h in range(heads):
        for copy in out_copies(h):
            copy.wait()


def on_device(sizes, q, k, v, x, top, gains):
    layers, blocks, shards = sizes
    rows, width = q.shape[1:]
    heads = width // HEAD
    padded = -(-rows // LANES) * LANES
    others, peers = max(layers - 1, 1), max(shards - 1, 1)
    wide = pltpu.VMEM((rows, width), BF16)
    wide32 = pltpu.VMEM((rows, width), F32)
    square = pltpu.VMEM((heads, HEAD, HEAD), BF16)
    dma = pltpu.SemaphoreType.DMA
    out = jax.ShapeDtypeStruct((1, rows, width), BF16)
    return pl.pallas_call(
        functools.partial(kernel, sizes),
        out_shape=(out,) * 4,
        in_specs=[pl.BlockSpec(memory_space=pl.ANY)] * 6,
        out_specs=(pl.BlockSpec(memory_space=pl.ANY),) * 4,
        scratch_shapes=[
            wide, wide, wide, wide, wide, pltpu.VMEM((1, width), F32),
            wide, wide, wide, wide,
            square, square, square, square,
            pltpu.VMEM((heads, HEAD, HEAD), F32),
            pltpu.VMEM((heads, rows, rows), BF16),
            wide32, wide32, wide32, wide,
            pltpu.VMEM((heads, rows, HEAD), BF16),
            pltpu.VMEM((others, heads, rows, HEAD), BF16),
            pltpu.VMEM((2, 8, padded), F32),
            pltpu.VMEM((2, peers, 8, padded), F32),
            pltpu.VMEM((8, padded), F32),
            pltpu.VMEM((others, 8, padded), F32),
            dma((6,)), dma, dma((3, heads)),
            dma((heads,)), dma((heads,)), dma((heads,)), dma((heads,)),
            dma((others, heads)), dma((others, heads)),
            dma((2, peers)), dma((2, peers)),
            dma((others,)), dma((others,)),
        ],
        compiler_params=pltpu.CompilerParams(collective_id=0, has_side_effects=True),
    )(q, k, v, x, top, gains)


def solution(mesh):
    sizes = (mesh.shape["pp"], mesh.shape["cp"], mesh.shape["tp"])
    part = P("pp", "cp", "tp")
    return jax.shard_map(
        functools.partial(on_device, sizes),
        mesh=mesh,
        in_specs=(part, part, part, part, P("cp", "tp"), P("pp", "tp")),
        out_specs=(part, part, part, part),
        check_vma=False,
    )
```

```python
import functools

import jax
import jax.numpy as jnp
from jax import lax
from jax.experimental import pallas as pl
from jax.experimental.pallas import tpu as pltpu
from jax.sharding import PartitionSpec as P

HEAD = 128
LANES = 128
EPSILON = 1e-06
GROUP = 2
VMEM_LIMIT = 24 << 20
MESH = pl.DeviceIdType.MESH
F32 = jnp.float32
BF16 = jnp.bfloat16


def dot(a, b, a_dim, b_dim):
    return lax.dot_general(a, b, (((a_dim,), (b_dim,)), ((), ())), preferred_element_type=F32)


def kernel(
    sizes,
    q_hbm, k_hbm, v_hbm, x_hbm, top_hbm, gain_hbm,
    outs,
    q, k, v, x, top, gain,
    pre_in, pre_out, suf_in, suf_out, states, scores, att, ng, gate, ag, b_out, b_in,
    rows_out, rows_in, inv_out, inv_in,
    in_sem, pre_send, pre_recv, suf_send, suf_recv,
    b_send, b_recv, row_send, row_recv, inv_send, inv_recv,
):
    layers, blocks, shards = sizes
    p = lax.axis_index("pp") if layers > 1 else jnp.int32(0)
    c = lax.axis_index("cp") if blocks > 1 else jnp.int32(0)
    t = lax.axis_index("tp") if shards > 1 else jnp.int32(0)
    rows, width = q.shape
    sec, qg, kg, vg = (outs.at[i] for i in range(4))
    heads = width // HEAD
    groups = [range(h, min(h + GROUP, heads)) for h in range(0, heads, GROUP)]
    padded = rows_out.shape[2]
    total_width = width * shards

    def cols(h):
        return slice(h * HEAD, (h + 1) * HEAD)

    loads = [
        pltpu.make_async_copy(k_hbm.at[0], k, in_sem.at[0]),
        pltpu.make_async_copy(v_hbm.at[0], v, in_sem.at[1]),
        pltpu.make_async_copy(q_hbm.at[0], q, in_sem.at[2]),
        pltpu.make_async_copy(x_hbm.at[0], x, in_sem.at[3]),
        pltpu.make_async_copy(gain_hbm, gain, in_sem.at[4]),
        pltpu.make_async_copy(top_hbm, top, in_sem.at[5]),
    ]
    for load in loads:
        load.start()

    barrier = pltpu.get_barrier_semaphore()

    @pl.when(c > 0)
    def _():
        pl.semaphore_signal(barrier, inc=1, device_id={"cp": c - 1}, device_id_type=MESH)

    @pl.when(c < blocks - 1)
    def _():
        pl.semaphore_signal(barrier, inc=1, device_id={"cp": c + 1}, device_id_type=MESH)

    for d in range(1, shards):
        pl.semaphore_signal(
            barrier, inc=1, device_id={"tp": lax.rem(t + d, shards)}, device_id_type=MESH
        )
    for d in range(1, layers):
        pl.semaphore_signal(
            barrier, inc=1, device_id={"pp": lax.rem(p + d, layers)}, device_id_type=MESH
        )

    @pl.when(c == 0)
    def _():
        pre_in[...] = jnp.zeros_like(pre_in)

    @pl.when(c == blocks - 1)
    def _():
        suf_in[...] = jnp.zeros_like(suf_in)

    for d in range(1, layers):

        @pl.when(p + d >= layers)
        def _():
            b_in[d - 1] = jnp.zeros(b_in.shape[1:], b_in.dtype)
            inv_in[d - 1] = jnp.zeros(inv_in.shape[1:], inv_in.dtype)

    def pre_copy(h):
        return pltpu.make_async_remote_copy(
            src_ref=pre_out.at[h], dst_ref=pre_in.at[h],
            send_sem=pre_send.at[h], recv_sem=pre_recv.at[h],
            device_id={"cp": c + 1}, device_id_type=MESH,
        )

    def suf_copy(h):
        return pltpu.make_async_remote_copy(
            src_ref=suf_out.at[h], dst_ref=suf_in.at[h],
            send_sem=suf_send.at[h], recv_sem=suf_recv.at[h],
            device_id={"cp": c - 1}, device_id_type=MESH,
        )

    def b_copy(d, h):
        return pltpu.make_async_remote_copy(
            src_ref=b_out.at[h], dst_ref=b_in.at[d - 1, h],
            send_sem=b_send.at[d - 1, h], recv_sem=b_recv.at[d - 1, h],
            device_id={"pp": p - d}, device_id_type=MESH,
        )

    def inv_copy(d):
        return pltpu.make_async_remote_copy(
            src_ref=inv_out, dst_ref=inv_in.at[d - 1],
            send_sem=inv_send.at[d - 1], recv_sem=inv_recv.at[d - 1],
            device_id={"pp": p - d}, device_id_type=MESH,
        )

    def row_copy(i, d):
        return pltpu.make_async_remote_copy(
            src_ref=rows_out.at[i], dst_ref=rows_in.at[i, d - 1],
            send_sem=row_send.at[i, d - 1], recv_sem=row_recv.at[i, d - 1],
            device_id={"tp": lax.rem(t + d, shards)}, device_id_type=MESH,
        )

    def to_row(partial):
        if padded > rows:
            fill = jnp.zeros((padded - rows, LANES), F32)
            partial = jnp.concatenate([partial, fill], axis=0)
        return jnp.broadcast_to(jnp.sum(partial.T, axis=0, keepdims=True), (8, padded))

    def to_col(row):
        return jnp.broadcast_to(row[0:1], (LANES, padded)).T[:rows]

    def row_start(i, partial):
        rows_out[i] = to_row(partial)
        for d in range(1, shards):
            row_copy(i, d).start()

    def row_finish(i):
        total = rows_out[i]
        for d in range(1, shards):
            row_copy(i, d).wait_recv()
            total = total + rows_in[i, d - 1]
        return total

    causal = lax.broadcasted_iota(jnp.int32, (rows, rows), 0) >= lax.broadcasted_iota(
        jnp.int32, (rows, rows), 1
    )

    partners = (shards - 1) + (layers - 1)
    pl.semaphore_wait(
        barrier, partners + jnp.where(c > 0, 1, 0) + jnp.where(c < blocks - 1, 1, 0)
    )

    loads[0].wait()
    loads[1].wait()
    for group in groups:
        for h in group:
            states[h] = dot(k[:, cols(h)], v[:, cols(h)], 0, 0)
        if blocks > 1:

            @pl.when(c == 0)
            def _():
                for h in group:
                    pre_out[h] = states[h].astype(BF16)
                    pre_copy(h).start()

    for load in loads[2:5]:
        load.wait()
    squares = jnp.zeros((rows, LANES), F32)
    for group in groups:
        for h in group:
            query, value = q[:, cols(h)], v[:, cols(h)]
            score = jnp.where(causal, dot(query, k[:, cols(h)], 1, 1), 0.0).astype(BF16)
            scores[h] = score
            att[:, cols(h)] = dot(score, value, 1, 0)
            gate[:, cols(h)] = jax.nn.sigmoid(x[:, cols(h)].astype(F32))
        if blocks > 1:

            @pl.when(c > 0)
            def _():
                for h in group:
                    pre_copy(h).wait_recv()

                    @pl.when(c < blocks - 1)
                    def _():
                        pre_out[h] = (pre_in[h].astype(F32) + states[h]).astype(BF16)
                        pre_copy(h).start()

        for h in group:
            attention = att[:, cols(h)] + dot(q[:, cols(h)], pre_in[h], 1, 0)
            att[:, cols(h)] = attention
            squares = squares + attention * attention
            if layers > 1:
                sig = gate[:, cols(h)]
                b_out[h] = (attention * (gain[:, cols(h)] * sig * (1.0 - sig))).astype(BF16)
        for d in range(1, layers):

            @pl.when(p >= d)
            def _():
                for h in group:
                    b_copy(d, h).start()

    row_start(0, squares)
    loads[5].wait()
    inv_row = 1.0 / jnp.sqrt(row_finish(0) / total_width + EPSILON)
    inv_out[...] = inv_row
    for d in range(1, layers):

        @pl.when(p >= d)
        def _():
            inv_copy(d).start()

    inv = to_col(inv_row)
    for d in range(1, layers):

        @pl.when(p + d < layers)
        def _():
            inv_copy(d).wait_recv()

    later_inv = [to_col(inv_in[d - 1]) for d in range(1, layers)]
    products = jnp.zeros((rows, LANES), F32)
    for h in range(heads):
        for d in range(1, layers):
            if h % GROUP == 0:

                @pl.when(p + d < layers)
                def _():
                    for near in range(h, min(h + GROUP, heads)):
                        b_copy(d, near).wait_recv()

        normed = att[:, cols(h)] * inv
        sig = gate[:, cols(h)]
        scaled = gain[:, cols(h)] * sig
        factor = 1.0 + normed * scaled * (1.0 - sig)
        incoming = top[:, cols(h)].astype(F32)
        for d in range(1, layers):

            incoming = incoming * (1.0 + b_in[d - 1, h].astype(F32) * later_inv[d - 1])
        sec[:, cols(h)] = (incoming * factor).astype(BF16)
        normed_grad = incoming * scaled
        ng[:, cols(h)] = normed_grad
        att[:, cols(h)] = normed
        products = products + normed_grad * normed

    row_start(1, products)
    mean = to_col(row_finish(1) / total_width)
    for group in groups:
        for h in group:
            grad = ((ng[:, cols(h)] - att[:, cols(h)] * mean) * inv).astype(BF16)
            ag[:, cols(h)] = grad
            states[h] = dot(q[:, cols(h)], grad, 0, 0)
        if blocks > 1:

            @pl.when(c == blocks - 1)
            def _():
                for h in group:
                    suf_out[h] = states[h].astype(BF16)
                    suf_copy(h).start()

    for group in groups:
        for h in group:
            query, key, value = q[:, cols(h)], k[:, cols(h)], v[:, cols(h)]
            grad = ag[:, cols(h)]
            score_grad = jnp.where(causal, dot(grad, value, 1, 1), 0.0).astype(BF16)
            query_grad = dot(score_grad, key, 1, 0) + dot(grad, pre_in[h], 1, 1)
            qg[:, cols(h)] = query_grad.astype(BF16)
            att[:, cols(h)] = dot(score_grad, query, 0, 0)
            ng[:, cols(h)] = dot(scores[h], grad, 0, 0)
        if blocks > 1:

            @pl.when(c < blocks - 1)
            def _():
                for h in group:
                    suf_copy(h).wait_recv()

                    @pl.when(c > 0)
                    def _():
                        suf_out[h] = (suf_in[h].astype(F32) + states[h]).astype(BF16)
                        suf_copy(h).start()

        for h in group:
            suffix = suf_in[h]
            key_grad = att[:, cols(h)] + dot(v[:, cols(h)], suffix, 1, 1)
            kg[:, cols(h)] = key_grad.astype(BF16)
            value_grad = ng[:, cols(h)] + dot(k[:, cols(h)], suffix, 1, 0)
            vg[:, cols(h)] = value_grad.astype(BF16)

    if blocks > 1:

        @pl.when(c < blocks - 1)
        def _():
            for h in range(heads):
                pre_copy(h).wait_send()

        @pl.when(c > 0)
        def _():
            for h in range(heads):
                suf_copy(h).wait_send()

    for d in range(1, layers):

        @pl.when(p >= d)
        def _():
            inv_copy(d).wait_send()
            for h in range(heads):
                b_copy(d, h).wait_send()

    for i in range(2):
        for d in range(1, shards):
            row_copy(i, d).wait_send()


def write_kernel(outs, sec_hbm, qg_hbm, kg_hbm, vg_hbm, sem):
    copies = [
        pltpu.make_async_copy(outs.at[i], dst.at[0], sem.at[i])
        for i, dst in enumerate((sec_hbm, qg_hbm, kg_hbm, vg_hbm))
    ]
    for copy in copies:
        copy.start()
    for copy in copies:
        copy.wait()


def on_device(sizes, q, k, v, x, top, gains):
    layers, blocks, shards = sizes
    rows, width = q.shape[1:]
    heads = width // HEAD
    padded = -(-rows // LANES) * LANES
    others, peers = max(layers - 1, 1), max(shards - 1, 1)
    wide = pltpu.VMEM((rows, width), BF16)
    wide32 = pltpu.VMEM((rows, width), F32)
    square = pltpu.VMEM((heads, HEAD, HEAD), BF16)
    dma = pltpu.SemaphoreType.DMA
    out = jax.ShapeDtypeStruct((1, rows, width), BF16)
    q, k, v, x, top, gains = (
        pltpu.with_memory_space_constraint(a, pltpu.HBM) for a in (q, k, v, x, top, gains)
    )
    outs = pl.pallas_call(
        functools.partial(kernel, sizes),
        out_shape=jax.ShapeDtypeStruct((4, rows, width), BF16),
        in_specs=[pl.BlockSpec(memory_space=pltpu.HBM)] * 6,
        out_specs=pl.BlockSpec(memory_space=pltpu.VMEM),
        scratch_shapes=[
            wide, wide, wide, wide, wide, pltpu.VMEM((1, width), F32),
            square, square, square, square,
            pltpu.VMEM((heads, HEAD, HEAD), F32),
            pltpu.VMEM((heads, rows, rows), BF16),
            wide32, wide32, wide32, wide,
            pltpu.VMEM((heads, rows, HEAD), BF16),
            pltpu.VMEM((others, heads, rows, HEAD), BF16),
            pltpu.VMEM((2, 8, padded), F32),
            pltpu.VMEM((2, peers, 8, padded), F32),
            pltpu.VMEM((8, padded), F32),
            pltpu.VMEM((others, 8, padded), F32),
            dma((6,)),
            dma((heads,)), dma((heads,)), dma((heads,)), dma((heads,)),
            dma((others, heads)), dma((others, heads)),
            dma((2, peers)), dma((2, peers)),
            dma((others,)), dma((others,)),
        ],
        compiler_params=pltpu.CompilerParams(collective_id=0, has_side_effects=True, vmem_limit_bytes=VMEM_LIMIT),
    )(q, k, v, x, top, gains)
    return pl.pallas_call(
        write_kernel,
        out_shape=(out,) * 4,
        in_specs=[pl.BlockSpec(memory_space=pltpu.VMEM)],
        out_specs=(pl.BlockSpec(memory_space=pl.ANY),) * 4,
        scratch_shapes=[dma((4,))],
        compiler_params=pltpu.CompilerParams(vmem_limit_bytes=1 << 20),
    )(outs)


def solution(mesh):
    sizes = (mesh.shape["pp"], mesh.shape["cp"], mesh.shape["tp"])
    part = P("pp", "cp", "tp")
    return jax.shard_map(
        functools.partial(on_device, sizes),
        mesh=mesh,
        in_specs=(part, part, part, part, P("cp", "tp"), P("pp", "tp")),
        out_specs=(part, part, part, part),
        check_vma=False,
    )
```

```python
import functools

import jax
import jax.numpy as jnp
from jax import lax
from jax.experimental import pallas as pl
from jax.experimental.pallas import tpu as pltpu
from jax.sharding import PartitionSpec as P

HEAD = 128
LANES = 128
EPSILON = 1e-06
GROUP = 2
PIECES = 1
VMEM_LIMIT = 24 << 20
MESH = pl.DeviceIdType.MESH
F32 = jnp.float32
BF16 = jnp.bfloat16


def dot(a, b, a_dim, b_dim):
    return lax.dot_general(a, b, (((a_dim,), (b_dim,)), ((), ())), preferred_element_type=F32)


def kernel(
    sizes,
    q_hbm, k_hbm, v_hbm, x_hbm, top_hbm, gain_hbm,
    outs,
    q, k, v, x, top, gain,
    pre_in, pre_out, suf_in, suf_out, states, scores, att, ng, gate, ag, b_out, b_in,
    rows_out, rows_in, inv_out, inv_in,
    in_sem, pre_send, pre_recv, suf_send, suf_recv,
    b_send, b_recv, row_send, row_recv, inv_send, inv_recv,
):
    layers, blocks, shards = sizes
    p = lax.axis_index("pp") if layers > 1 else jnp.int32(0)
    c = lax.axis_index("cp") if blocks > 1 else jnp.int32(0)
    t = lax.axis_index("tp") if shards > 1 else jnp.int32(0)
    rows, width = q.shape
    sec, qg, kg, vg = (outs.at[i] for i in range(4))
    heads = width // HEAD
    groups = [range(h, min(h + GROUP, heads)) for h in range(0, heads, GROUP)]
    padded = rows_out.shape[2]
    total_width = width * shards

    def part(i):
        return slice(i * (HEAD // PIECES), (i + 1) * (HEAD // PIECES))

    def pieces(group):
        return [(h, i) for h in group for i in range(PIECES)]

    def cols(h):
        return slice(h * HEAD, (h + 1) * HEAD)

    loads = [
        pltpu.make_async_copy(k_hbm.at[0], k, in_sem.at[0]),
        pltpu.make_async_copy(v_hbm.at[0], v, in_sem.at[1]),
        pltpu.make_async_copy(q_hbm.at[0], q, in_sem.at[2]),
        pltpu.make_async_copy(x_hbm.at[0], x, in_sem.at[3]),
        pltpu.make_async_copy(gain_hbm, gain, in_sem.at[4]),
        pltpu.make_async_copy(top_hbm, top, in_sem.at[5]),
    ]
    for load in loads[:2]:
        load.start()

    barrier = pltpu.get_barrier_semaphore()

    @pl.when(c > 0)
    def _():
        pl.semaphore_signal(barrier, inc=1, device_id={"cp": c - 1}, device_id_type=MESH)

    @pl.when(c < blocks - 1)
    def _():
        pl.semaphore_signal(barrier, inc=1, device_id={"cp": c + 1}, device_id_type=MESH)

    for d in range(1, shards):
        pl.semaphore_signal(
            barrier, inc=1, device_id={"tp": lax.rem(t + d, shards)}, device_id_type=MESH
        )
    for d in range(1, layers):
        pl.semaphore_signal(
            barrier, inc=1, device_id={"pp": lax.rem(p + d, layers)}, device_id_type=MESH
        )

    @pl.when(c == 0)
    def _():
        pre_in[...] = jnp.zeros_like(pre_in)

    @pl.when(c == blocks - 1)
    def _():
        suf_in[...] = jnp.zeros_like(suf_in)

    for d in range(1, layers):

        @pl.when(p + d >= layers)
        def _():
            b_in[d - 1] = jnp.zeros(b_in.shape[1:], b_in.dtype)
            inv_in[d - 1] = jnp.zeros(inv_in.shape[1:], inv_in.dtype)

    def pre_copy(h, i):
        return pltpu.make_async_remote_copy(
            src_ref=pre_out.at[h, part(i)], dst_ref=pre_in.at[h, part(i)],
            send_sem=pre_send.at[h, i], recv_sem=pre_recv.at[h, i],
            device_id={"cp": c + 1}, device_id_type=MESH,
        )

    def suf_copy(h, i):
        return pltpu.make_async_remote_copy(
            src_ref=suf_out.at[h, part(i)], dst_ref=suf_in.at[h, part(i)],
            send_sem=suf_send.at[h, i], recv_sem=suf_recv.at[h, i],
            device_id={"cp": c - 1}, device_id_type=MESH,
        )

    def b_copy(d, h):
        return pltpu.make_async_remote_copy(
            src_ref=b_out.at[h], dst_ref=b_in.at[d - 1, h],
            send_sem=b_send.at[d - 1, h], recv_sem=b_recv.at[d - 1, h],
            device_id={"pp": p - d}, device_id_type=MESH,
        )

    def inv_copy(d):
        return pltpu.make_async_remote_copy(
            src_ref=inv_out, dst_ref=inv_in.at[d - 1],
            send_sem=inv_send.at[d - 1], recv_sem=inv_recv.at[d - 1],
            device_id={"pp": p - d}, device_id_type=MESH,
        )

    def row_copy(i, d):
        return pltpu.make_async_remote_copy(
            src_ref=rows_out.at[i], dst_ref=rows_in.at[i, d - 1],
            send_sem=row_send.at[i, d - 1], recv_sem=row_recv.at[i, d - 1],
            device_id={"tp": lax.rem(t + d, shards)}, device_id_type=MESH,
        )

    def to_row(partial):
        if padded > rows:
            fill = jnp.zeros((padded - rows, LANES), F32)
            partial = jnp.concatenate([partial, fill], axis=0)
        return jnp.broadcast_to(jnp.sum(partial.T, axis=0, keepdims=True), (8, padded))

    def to_col(row):
        return jnp.broadcast_to(row[0:1], (LANES, padded)).T[:rows]

    def row_start(i, partials):
        ids = lax.broadcasted_iota(jnp.int32, (8, padded), 0)
        packed = to_row(partials[0])
        for j in range(1, len(partials)):
            packed = jnp.where(ids == j, to_row(partials[j]), packed)
        rows_out[i] = packed
        for d in range(1, shards):
            row_copy(i, d).start()

    def row_finish(i):
        total = rows_out[i]
        for d in range(1, shards):
            row_copy(i, d).wait_recv()
            total = total + rows_in[i, d - 1]
        return total

    causal = lax.broadcasted_iota(jnp.int32, (rows, rows), 0) >= lax.broadcasted_iota(
        jnp.int32, (rows, rows), 1
    )

    partners = (shards - 1) + (layers - 1)
    pl.semaphore_wait(
        barrier, partners + jnp.where(c > 0, 1, 0) + jnp.where(c < blocks - 1, 1, 0)
    )

    loads[0].wait()
    loads[1].wait()
    for load in loads[2:]:
        load.start()
    for group in groups:
        for h in group:
            states[h] = dot(k[:, cols(h)], v[:, cols(h)], 0, 0)
        if blocks > 1:

            @pl.when(c == 0)
            def _():
                for h in group:
                    for i in range(PIECES):
                        pre_out[h, part(i)] = states[h, part(i)].astype(BF16)
                        pre_copy(h, i).start()

    for load in loads[2:]:
        load.wait()
    merged = layers <= 2
    squares = jnp.zeros((rows, LANES), F32)
    firsts = jnp.zeros((rows, LANES), F32)
    for group in groups:
        for h in group:
            query, value = q[:, cols(h)], v[:, cols(h)]
            score = jnp.where(causal, dot(query, k[:, cols(h)], 1, 1), 0.0).astype(BF16)
            scores[h] = score
            att[:, cols(h)] = dot(score, value, 1, 0)
            gate[:, cols(h)] = jax.nn.sigmoid(x[:, cols(h)].astype(F32))
        if blocks > 1:

            @pl.when(c > 0)
            def _():
                for h, i in pieces(group):
                    pre_copy(h, i).wait_recv()

                    @pl.when(c < blocks - 1)
                    def _():
                        total = pre_in[h, part(i)].astype(F32) + states[h, part(i)]
                        pre_out[h, part(i)] = total.astype(BF16)
                        pre_copy(h, i).start()

        for h in group:
            attention = att[:, cols(h)] + dot(q[:, cols(h)], pre_in[h], 1, 0)
            att[:, cols(h)] = attention
            squares = squares + attention * attention
            sig = gate[:, cols(h)]
            if merged:
                weighted = top[:, cols(h)].astype(F32) * (gain[:, cols(h)] * sig)
                ng[:, cols(h)] = weighted
                firsts = firsts + weighted * attention
            if layers > 1:
                b_out[h] = (attention * (gain[:, cols(h)] * sig * (1.0 - sig))).astype(BF16)
        for d in range(1, layers):

            @pl.when(p >= d)
            def _():
                for h in group:
                    b_copy(d, h).start()

    row_start(0, (squares, firsts))
    sums = row_finish(0)
    inv_row = 1.0 / jnp.sqrt(sums[0:1] / total_width + EPSILON)
    inv_out[...] = jnp.broadcast_to(inv_row, inv_out.shape)
    for d in range(1, layers):

        @pl.when(p >= d)
        def _():
            inv_copy(d).start()

    inv = to_col(inv_row)

    def wait_inv():
        for d in range(1, layers):

            @pl.when(p + d < layers)
            def _():
                inv_copy(d).wait_recv()

    def wait_b(group):
        for d in range(1, layers):

            @pl.when(p + d < layers)
            def _():
                for h in group:
                    b_copy(d, h).wait_recv()

    def later(h, later_inv):
        incoming = top[:, cols(h)].astype(F32)
        for d in range(1, layers):
            incoming = incoming * (1.0 + b_in[d - 1, h].astype(F32) * later_inv[d - 1])
        return incoming

    if merged:
        mean_row = sums[1:2]
        if layers > 1:
            seconds = jnp.zeros((rows, LANES), F32)
            for group in groups:
                wait_b(group)
                for h in group:
                    seconds = seconds + ng[:, cols(h)] * att[:, cols(h)] * b_in[0, h].astype(F32)

            @pl.when(p < layers - 1)
            def _():
                row_start(1, (seconds,))
                wait_inv()
                total = row_finish(1)
                for d in range(1, shards):
                    row_copy(1, d).wait_send()
                rows_out[1] = total

            @pl.when(p == layers - 1)
            def _():
                rows_out[1] = jnp.zeros(rows_out.shape[1:], F32)

            mean_row = mean_row + inv_in[0, 0:1] * rows_out[1, 0:1]
        mean_row = mean_row * inv_row
        later_inv = [to_col(inv_in[d - 1]) for d in range(1, layers)]
    else:
        wait_inv()
        later_inv = [to_col(inv_in[d - 1]) for d in range(1, layers)]
        products = jnp.zeros((rows, LANES), F32)
        for group in groups:
            wait_b(group)
            for h in group:
                weighted = later(h, later_inv) * (gain[:, cols(h)] * gate[:, cols(h)])
                ng[:, cols(h)] = weighted
                products = products + weighted * att[:, cols(h)] * inv
        row_start(1, (products,))
        mean_row = row_finish(1)
    mean = to_col(mean_row / total_width)
    for group in groups:
        for h in group:
            weighted = ng[:, cols(h)]
            if merged and layers > 1:
                weighted = weighted * (1.0 + b_in[0, h].astype(F32) * later_inv[0])
            grad = ((weighted - att[:, cols(h)] * inv * mean) * inv).astype(BF16)
            ag[:, cols(h)] = grad
            states[h] = dot(q[:, cols(h)], grad, 0, 0)
        if blocks > 1:

            @pl.when(c == blocks - 1)
            def _():
                for h in group:
                    for i in range(PIECES):
                        suf_out[h, part(i)] = states[h, part(i)].astype(BF16)
                        suf_copy(h, i).start()

    for group in groups:
        for h in group:
            sig = gate[:, cols(h)]
            slope = gain[:, cols(h)] * sig * (1.0 - sig)
            factor = 1.0 + att[:, cols(h)] * inv * slope
            sec[:, cols(h)] = (later(h, later_inv) * factor).astype(BF16)
            query, key, value = q[:, cols(h)], k[:, cols(h)], v[:, cols(h)]
            grad = ag[:, cols(h)]
            score_grad = jnp.where(causal, dot(grad, value, 1, 1), 0.0).astype(BF16)
            query_grad = dot(score_grad, key, 1, 0) + dot(grad, pre_in[h], 1, 1)
            qg[:, cols(h)] = query_grad.astype(BF16)
            att[:, cols(h)] = dot(score_grad, query, 0, 0)
            ng[:, cols(h)] = dot(scores[h], grad, 0, 0)
        if blocks > 1:

            @pl.when(c < blocks - 1)
            def _():
                for h, i in pieces(group):
                    suf_copy(h, i).wait_recv()

                    @pl.when(c > 0)
                    def _():
                        total = suf_in[h, part(i)].astype(F32) + states[h, part(i)]
                        suf_out[h, part(i)] = total.astype(BF16)
                        suf_copy(h, i).start()

        for h in group:
            suffix = suf_in[h]
            key_grad = att[:, cols(h)] + dot(v[:, cols(h)], suffix, 1, 1)
            kg[:, cols(h)] = key_grad.astype(BF16)
            value_grad = ng[:, cols(h)] + dot(k[:, cols(h)], suffix, 1, 0)
            vg[:, cols(h)] = value_grad.astype(BF16)

    if blocks > 1:

        @pl.when(c < blocks - 1)
        def _():
            for h, i in pieces(range(heads)):
                pre_copy(h, i).wait_send()

        @pl.when(c > 0)
        def _():
            for h, i in pieces(range(heads)):
                suf_copy(h, i).wait_send()

    for d in range(1, layers):

        @pl.when(p >= d)
        def _():
            inv_copy(d).wait_send()
            for h in range(heads):
                b_copy(d, h).wait_send()

    for d in range(1, shards):
        row_copy(0, d).wait_send()
    if not merged:
        for d in range(1, shards):
            row_copy(1, d).wait_send()


def write_kernel(outs, sec_hbm, qg_hbm, kg_hbm, vg_hbm, sem):
    copies = [
        pltpu.make_async_copy(outs.at[i], dst.at[0], sem.at[i])
        for i, dst in enumerate((sec_hbm, qg_hbm, kg_hbm, vg_hbm))
    ]
    for copy in copies:
        copy.start()
    for copy in copies:
        copy.wait()


def on_device(sizes, q, k, v, x, top, gains):
    layers, blocks, shards = sizes
    rows, width = q.shape[1:]
    heads = width // HEAD
    padded = -(-rows // LANES) * LANES
    others, peers = max(layers - 1, 1), max(shards - 1, 1)
    wide = pltpu.VMEM((rows, width), BF16)
    wide32 = pltpu.VMEM((rows, width), F32)
    square = pltpu.VMEM((heads, HEAD, HEAD), BF16)
    dma = pltpu.SemaphoreType.DMA
    chain = dma((heads, PIECES))
    out = jax.ShapeDtypeStruct((1, rows, width), BF16)
    q, k, v, x, top, gains = (
        pltpu.with_memory_space_constraint(a, pltpu.HBM) for a in (q, k, v, x, top, gains)
    )
    outs = pl.pallas_call(
        functools.partial(kernel, sizes),
        out_shape=jax.ShapeDtypeStruct((4, rows, width), BF16),
        in_specs=[pl.BlockSpec(memory_space=pltpu.HBM)] * 6,
        out_specs=pl.BlockSpec(memory_space=pltpu.VMEM),
        scratch_shapes=[
            wide, wide, wide, wide, wide, pltpu.VMEM((1, width), F32),
            square, square, square, square,
            pltpu.VMEM((heads, HEAD, HEAD), F32),
            pltpu.VMEM((heads, rows, rows), BF16),
            wide32, wide32, wide32, wide,
            pltpu.VMEM((heads, rows, HEAD), BF16),
            pltpu.VMEM((others, heads, rows, HEAD), BF16),
            pltpu.VMEM((2, 8, padded), F32),
            pltpu.VMEM((2, peers, 8, padded), F32),
            pltpu.VMEM((8, padded), F32),
            pltpu.VMEM((others, 8, padded), F32),
            dma((6,)),
            chain, chain, chain, chain,
            dma((others, heads)), dma((others, heads)),
            dma((2, peers)), dma((2, peers)),
            dma((others,)), dma((others,)),
        ],
        compiler_params=pltpu.CompilerParams(collective_id=0, has_side_effects=True, vmem_limit_bytes=VMEM_LIMIT),
    )(q, k, v, x, top, gains)
    return pl.pallas_call(
        write_kernel,
        out_shape=(out,) * 4,
        in_specs=[pl.BlockSpec(memory_space=pltpu.VMEM)],
        out_specs=(pl.BlockSpec(memory_space=pl.ANY),) * 4,
        scratch_shapes=[dma((4,))],
        compiler_params=pltpu.CompilerParams(vmem_limit_bytes=1 << 20),
    )(outs)


def solution(mesh):
    sizes = (mesh.shape["pp"], mesh.shape["cp"], mesh.shape["tp"])
    part = P("pp", "cp", "tp")
    return jax.shard_map(
        functools.partial(on_device, sizes),
        mesh=mesh,
        in_specs=(part, part, part, part, P("cp", "tp"), P("pp", "tp")),
        out_specs=(part, part, part, part),
        check_vma=False,
    )
```

```python
import functools

import jax
import jax.numpy as jnp
from jax import lax
from jax.experimental import pallas as pl
from jax.experimental.pallas import tpu as pltpu
from jax.sharding import PartitionSpec as P

HEAD = 128
LANES = 128
EPSILON = 1e-06
GROUP = 1
PIECES = 1
VMEM_LIMIT = 24 << 20
MESH = pl.DeviceIdType.MESH
F32 = jnp.float32
BF16 = jnp.bfloat16


def dot(a, b, a_dim, b_dim):
    return lax.dot_general(a, b, (((a_dim,), (b_dim,)), ((), ())), preferred_element_type=F32)


def kernel(
    sizes,
    q_hbm, k_hbm, v_hbm, x_hbm, top_hbm, gain_hbm,
    outs,
    q, k, v, x, top, gain,
    pre_in, pre_out, suf_in, suf_out, states, scores, att, ng, gate, ag, b_out, b_in,
    rows_out, rows_in, inv_out, inv_in,
    in_sem, pre_send, pre_recv, suf_send, suf_recv,
    b_send, b_recv, row_send, row_recv, inv_send, inv_recv,
):
    layers, blocks, shards = sizes
    p = lax.axis_index("pp") if layers > 1 else jnp.int32(0)
    c = lax.axis_index("cp") if blocks > 1 else jnp.int32(0)
    t = lax.axis_index("tp") if shards > 1 else jnp.int32(0)
    rows, width = q.shape
    sec, qg, kg, vg = (outs.at[i] for i in range(4))
    heads = width // HEAD
    groups = [range(h, min(h + GROUP, heads)) for h in range(0, heads, GROUP)]
    padded = rows_out.shape[2]
    total_width = width * shards

    def part(i):
        return slice(i * (HEAD // PIECES), (i + 1) * (HEAD // PIECES))

    def pieces(group):
        return [(h, i) for h in group for i in range(PIECES)]

    def cols(h):
        return slice(h * HEAD, (h + 1) * HEAD)

    loads = [
        pltpu.make_async_copy(k_hbm.at[0], k, in_sem.at[0]),
        pltpu.make_async_copy(v_hbm.at[0], v, in_sem.at[1]),
        pltpu.make_async_copy(q_hbm.at[0], q, in_sem.at[2]),
        pltpu.make_async_copy(x_hbm.at[0], x, in_sem.at[3]),
        pltpu.make_async_copy(gain_hbm, gain, in_sem.at[4]),
        pltpu.make_async_copy(top_hbm, top, in_sem.at[5]),
    ]
    for load in loads[:2]:
        load.start()

    barrier = pltpu.get_barrier_semaphore()

    @pl.when(c > 0)
    def _():
        pl.semaphore_signal(barrier, inc=1, device_id={"cp": c - 1}, device_id_type=MESH)

    @pl.when(c < blocks - 1)
    def _():
        pl.semaphore_signal(barrier, inc=1, device_id={"cp": c + 1}, device_id_type=MESH)

    for d in range(1, shards):
        pl.semaphore_signal(
            barrier, inc=1, device_id={"tp": lax.rem(t + d, shards)}, device_id_type=MESH
        )
    for d in range(1, layers):
        pl.semaphore_signal(
            barrier, inc=1, device_id={"pp": lax.rem(p + d, layers)}, device_id_type=MESH
        )

    @pl.when(c == 0)
    def _():
        pre_in[...] = jnp.zeros_like(pre_in)

    @pl.when(c == blocks - 1)
    def _():
        suf_in[...] = jnp.zeros_like(suf_in)

    for d in range(1, layers):

        @pl.when(p + d >= layers)
        def _():
            b_in[d - 1] = jnp.zeros(b_in.shape[1:], b_in.dtype)
            inv_in[d - 1] = jnp.zeros(inv_in.shape[1:], inv_in.dtype)

    def pre_copy(h, i):
        return pltpu.make_async_remote_copy(
            src_ref=pre_out.at[h, part(i)], dst_ref=pre_in.at[h, part(i)],
            send_sem=pre_send.at[h, i], recv_sem=pre_recv.at[h, i],
            device_id={"cp": c + 1}, device_id_type=MESH,
        )

    def suf_copy(h, i):
        return pltpu.make_async_remote_copy(
            src_ref=suf_out.at[h, part(i)], dst_ref=suf_in.at[h, part(i)],
            send_sem=suf_send.at[h, i], recv_sem=suf_recv.at[h, i],
            device_id={"cp": c - 1}, device_id_type=MESH,
        )

    def b_copy(d, h):
        return pltpu.make_async_remote_copy(
            src_ref=b_out.at[h], dst_ref=b_in.at[d - 1, h],
            send_sem=b_send.at[d - 1, h], recv_sem=b_recv.at[d - 1, h],
            device_id={"pp": p - d}, device_id_type=MESH,
        )

    def inv_copy(d):
        return pltpu.make_async_remote_copy(
            src_ref=inv_out, dst_ref=inv_in.at[d - 1],
            send_sem=inv_send.at[d - 1], recv_sem=inv_recv.at[d - 1],
            device_id={"pp": p - d}, device_id_type=MESH,
        )

    def row_copy(i, d):
        return pltpu.make_async_remote_copy(
            src_ref=rows_out.at[i], dst_ref=rows_in.at[i, d - 1],
            send_sem=row_send.at[i, d - 1], recv_sem=row_recv.at[i, d - 1],
            device_id={"tp": lax.rem(t + d, shards)}, device_id_type=MESH,
        )

    def to_row(partial):
        if padded > rows:
            fill = jnp.zeros((padded - rows, LANES), F32)
            partial = jnp.concatenate([partial, fill], axis=0)
        return jnp.broadcast_to(jnp.sum(partial.T, axis=0, keepdims=True), (8, padded))

    def to_col(row):
        return jnp.broadcast_to(row[0:1], (LANES, padded)).T[:rows]

    def row_start(i, partials):
        ids = lax.broadcasted_iota(jnp.int32, (8, padded), 0)
        packed = to_row(partials[0])
        for j in range(1, len(partials)):
            packed = jnp.where(ids == j, to_row(partials[j]), packed)
        rows_out[i] = packed
        for d in range(1, shards):
            row_copy(i, d).start()

    def row_finish(i):
        total = rows_out[i]
        for d in range(1, shards):
            row_copy(i, d).wait_recv()
            total = total + rows_in[i, d - 1]
        return total

    causal = lax.broadcasted_iota(jnp.int32, (rows, rows), 0) >= lax.broadcasted_iota(
        jnp.int32, (rows, rows), 1
    )

    partners = (shards - 1) + (layers - 1)
    pl.semaphore_wait(
        barrier, partners + jnp.where(c > 0, 1, 0) + jnp.where(c < blocks - 1, 1, 0)
    )

    loads[0].wait()
    loads[1].wait()
    for load in loads[2:]:
        load.start()
    for group in groups:
        for h in group:
            states[h] = dot(k[:, cols(h)], v[:, cols(h)], 0, 0)
        if blocks > 1:

            @pl.when(c == 0)
            def _():
                for h in group:
                    for i in range(PIECES):
                        pre_out[h, part(i)] = states[h, part(i)].astype(BF16)
                        pre_copy(h, i).start()

    for load in loads[2:]:
        load.wait()
    merged = layers <= 2
    squares = jnp.zeros((rows, LANES), F32)
    firsts = jnp.zeros((rows, LANES), F32)
    for group in groups:
        for h in group:
            query, value = q[:, cols(h)], v[:, cols(h)]
            score = jnp.where(causal, dot(query, k[:, cols(h)], 1, 1), 0.0).astype(BF16)
            scores[h] = score
            att[:, cols(h)] = dot(score, value, 1, 0)
            gate[:, cols(h)] = jax.nn.sigmoid(x[:, cols(h)].astype(F32))
        if blocks > 1:

            @pl.when(c > 0)
            def _():
                for h, i in pieces(group):
                    pre_copy(h, i).wait_recv()

                    @pl.when(c < blocks - 1)
                    def _():
                        total = pre_in[h, part(i)].astype(F32) + states[h, part(i)]
                        pre_out[h, part(i)] = total.astype(BF16)
                        pre_copy(h, i).start()

        for h in group:
            attention = att[:, cols(h)] + dot(q[:, cols(h)], pre_in[h], 1, 0)
            att[:, cols(h)] = attention
            squares = squares + attention * attention
            sig = gate[:, cols(h)]
            if merged:
                weighted = top[:, cols(h)].astype(F32) * (gain[:, cols(h)] * sig)
                ng[:, cols(h)] = weighted
                firsts = firsts + weighted * attention
            if layers > 1:
                b_out[h] = (attention * (gain[:, cols(h)] * sig * (1.0 - sig))).astype(BF16)
        for d in range(1, layers):

            @pl.when(p >= d)
            def _():
                for h in group:
                    b_copy(d, h).start()

    row_start(0, (squares, firsts))
    sums = row_finish(0)
    inv_row = 1.0 / jnp.sqrt(sums[0:1] / total_width + EPSILON)
    inv_out[...] = jnp.broadcast_to(inv_row, inv_out.shape)
    for d in range(1, layers):

        @pl.when(p >= d)
        def _():
            inv_copy(d).start()

    inv = to_col(inv_row)

    def wait_inv():
        for d in range(1, layers):

            @pl.when(p + d < layers)
            def _():
                inv_copy(d).wait_recv()

    def wait_b(group):
        for d in range(1, layers):

            @pl.when(p + d < layers)
            def _():
                for h in group:
                    b_copy(d, h).wait_recv()

    def later(h, later_inv):
        incoming = top[:, cols(h)].astype(F32)
        for d in range(1, layers):
            incoming = incoming * (1.0 + b_in[d - 1, h].astype(F32) * later_inv[d - 1])
        return incoming

    if merged:
        mean_row = sums[1:2]
        if layers > 1:
            seconds = jnp.zeros((rows, LANES), F32)
            for group in groups:
                wait_b(group)
                for h in group:
                    seconds = seconds + ng[:, cols(h)] * att[:, cols(h)] * b_in[0, h].astype(F32)

            @pl.when(p < layers - 1)
            def _():
                row_start(1, (seconds,))
                wait_inv()
                total = row_finish(1)
                for d in range(1, shards):
                    row_copy(1, d).wait_send()
                rows_out[1] = total

            @pl.when(p == layers - 1)
            def _():
                rows_out[1] = jnp.zeros(rows_out.shape[1:], F32)

            mean_row = mean_row + inv_in[0, 0:1] * rows_out[1, 0:1]
        mean_row = mean_row * inv_row
        later_inv = [to_col(inv_in[d - 1]) for d in range(1, layers)]
    else:
        wait_inv()
        later_inv = [to_col(inv_in[d - 1]) for d in range(1, layers)]
        products = jnp.zeros((rows, LANES), F32)
        for group in groups:
            wait_b(group)
            for h in group:
                weighted = later(h, later_inv) * (gain[:, cols(h)] * gate[:, cols(h)])
                ng[:, cols(h)] = weighted
                products = products + weighted * att[:, cols(h)] * inv
        row_start(1, (products,))
        mean_row = row_finish(1)
    mean = to_col(mean_row / total_width)
    for group in groups:
        for h in group:
            weighted = ng[:, cols(h)]
            if merged and layers > 1:
                weighted = weighted * (1.0 + b_in[0, h].astype(F32) * later_inv[0])
            grad = ((weighted - att[:, cols(h)] * inv * mean) * inv).astype(BF16)
            ag[:, cols(h)] = grad
            states[h] = dot(q[:, cols(h)], grad, 0, 0)
        if blocks > 1:

            @pl.when(c == blocks - 1)
            def _():
                for h in group:
                    for i in range(PIECES):
                        suf_out[h, part(i)] = states[h, part(i)].astype(BF16)
                        suf_copy(h, i).start()

    for group in groups:
        for h in group:
            sig = gate[:, cols(h)]
            slope = gain[:, cols(h)] * sig * (1.0 - sig)
            factor = 1.0 + att[:, cols(h)] * inv * slope
            sec[:, cols(h)] = (later(h, later_inv) * factor).astype(BF16)
            query, key, value = q[:, cols(h)], k[:, cols(h)], v[:, cols(h)]
            grad = ag[:, cols(h)]
            score_grad = jnp.where(causal, dot(grad, value, 1, 1), 0.0).astype(BF16)
            query_grad = dot(score_grad, key, 1, 0) + dot(grad, pre_in[h], 1, 1)
            qg[:, cols(h)] = query_grad.astype(BF16)
            att[:, cols(h)] = dot(score_grad, query, 0, 0)
            ng[:, cols(h)] = dot(scores[h], grad, 0, 0)
        if blocks > 1:

            @pl.when(c < blocks - 1)
            def _():
                for h, i in pieces(group):
                    suf_copy(h, i).wait_recv()

                    @pl.when(c > 0)
                    def _():
                        total = suf_in[h, part(i)].astype(F32) + states[h, part(i)]
                        suf_out[h, part(i)] = total.astype(BF16)
                        suf_copy(h, i).start()

        for h in group:
            suffix = suf_in[h]
            key_grad = att[:, cols(h)] + dot(v[:, cols(h)], suffix, 1, 1)
            kg[:, cols(h)] = key_grad.astype(BF16)
            value_grad = ng[:, cols(h)] + dot(k[:, cols(h)], suffix, 1, 0)
            vg[:, cols(h)] = value_grad.astype(BF16)

    if blocks > 1:

        @pl.when(c < blocks - 1)
        def _():
            for h, i in pieces(range(heads)):
                pre_copy(h, i).wait_send()

        @pl.when(c > 0)
        def _():
            for h, i in pieces(range(heads)):
                suf_copy(h, i).wait_send()

    for d in range(1, layers):

        @pl.when(p >= d)
        def _():
            inv_copy(d).wait_send()
            for h in range(heads):
                b_copy(d, h).wait_send()

    for d in range(1, shards):
        row_copy(0, d).wait_send()
    if not merged:
        for d in range(1, shards):
            row_copy(1, d).wait_send()


def write_kernel(outs, sec_hbm, qg_hbm, kg_hbm, vg_hbm, sem):
    copies = [
        pltpu.make_async_copy(outs.at[i], dst.at[0], sem.at[i])
        for i, dst in enumerate((sec_hbm, qg_hbm, kg_hbm, vg_hbm))
    ]
    for copy in copies:
        copy.start()
    for copy in copies:
        copy.wait()


def on_device(sizes, q, k, v, x, top, gains):
    layers, blocks, shards = sizes
    rows, width = q.shape[1:]
    heads = width // HEAD
    padded = -(-rows // LANES) * LANES
    others, peers = max(layers - 1, 1), max(shards - 1, 1)
    wide = pltpu.VMEM((rows, width), BF16)
    wide32 = pltpu.VMEM((rows, width), F32)
    square = pltpu.VMEM((heads, HEAD, HEAD), BF16)
    dma = pltpu.SemaphoreType.DMA
    chain = dma((heads, PIECES))
    out = jax.ShapeDtypeStruct((1, rows, width), BF16)
    q, k, v, x, top, gains = (
        pltpu.with_memory_space_constraint(a, pltpu.HBM) for a in (q, k, v, x, top, gains)
    )
    outs = pl.pallas_call(
        functools.partial(kernel, sizes),
        out_shape=jax.ShapeDtypeStruct((4, rows, width), BF16),
        in_specs=[pl.BlockSpec(memory_space=pltpu.HBM)] * 6,
        out_specs=pl.BlockSpec(memory_space=pltpu.VMEM),
        scratch_shapes=[
            wide, wide, wide, wide, wide, pltpu.VMEM((1, width), F32),
            square, square, square, square,
            pltpu.VMEM((heads, HEAD, HEAD), F32),
            pltpu.VMEM((heads, rows, rows), BF16),
            wide32, wide32, wide32, wide,
            pltpu.VMEM((heads, rows, HEAD), BF16),
            pltpu.VMEM((others, heads, rows, HEAD), BF16),
            pltpu.VMEM((2, 8, padded), F32),
            pltpu.VMEM((2, peers, 8, padded), F32),
            pltpu.VMEM((8, padded), F32),
            pltpu.VMEM((others, 8, padded), F32),
            dma((6,)),
            chain, chain, chain, chain,
            dma((others, heads)), dma((others, heads)),
            dma((2, peers)), dma((2, peers)),
            dma((others,)), dma((others,)),
        ],
        compiler_params=pltpu.CompilerParams(collective_id=0, has_side_effects=True, vmem_limit_bytes=VMEM_LIMIT),
    )(q, k, v, x, top, gains)
    return pl.pallas_call(
        write_kernel,
        out_shape=(out,) * 4,
        in_specs=[pl.BlockSpec(memory_space=pltpu.VMEM)],
        out_specs=(pl.BlockSpec(memory_space=pl.ANY),) * 4,
        scratch_shapes=[dma((4,))],
        compiler_params=pltpu.CompilerParams(vmem_limit_bytes=1 << 20),
    )(outs)


def solution(mesh):
    sizes = (mesh.shape["pp"], mesh.shape["cp"], mesh.shape["tp"])
    part = P("pp", "cp", "tp")
    return jax.shard_map(
        functools.partial(on_device, sizes),
        mesh=mesh,
        in_specs=(part, part, part, part, P("cp", "tp"), P("pp", "tp")),
        out_specs=(part, part, part, part),
        check_vma=False,
    )
```
